512 devices in a mesh: dp: 16 (over z, core), space: 32 (over x, y).
Axes of the slice: x: 4, y: 8, z: 8, core: 2. Of those that a mesh axis runs over, the one named last changes fastest.
Arguments:
- features: bfloat16 [16, 32, 128, 32, 128], P('dp', None, 'space'), may hold values from -6 to 6
- cotangent: bfloat16 [16, 32, 128, 32, 128], P('dp', None, 'space'), may hold values from -6 to 6
- spectral: bfloat16 [256, 32, 2048], P('space', 'dp'), may hold values from -3 to 3
- pointwise: bfloat16 [32, 32], replicated, may hold values from -1 to 1
- biases: bfloat16 [32], replicated, may hold values from -3 to 3
Outputs:
- grad_input: bfloat16 [16, 32, 128, 32, 128], P('dp', None, 'space')
- grad_spectral: float32 [256, 32, 2048], P('space', 'dp')
The draws below stay inside these ranges and needn't reach their ends.
All inputs are finite; a program needn't handle non-finite values.
Results may differ from the reference program's by a relative error of at most 0.025.
Values may be sent and summed in bfloat16 or wider, within the bound.
No kernel may reach another device: no remote copies, remote signals or barrier semaphores. Data moves between devices by JAX's collectives and lax.ppermute only.
A program may use at most 64 MiB of HBM per device.

```python
import math
import jax
import jax.numpy as jnp
from jax import lax

C = 32
KX = 32
KY = 32
KZ = 8
NY = 32
NZ = 128
NX = 128
SAMPLES = 16


def levels(rng, dims, cuts, least, high):
    gain, own = 1.0, jax.random.fold_in(rng, 6)
    for axis_at, parts in cuts:
        heights = jnp.exp(jax.random.uniform(jax.random.fold_in(own, axis_at), (parts,), jnp.float32, least / len(cuts), high / len(cuts)))
        gain = gain * jnp.repeat(heights, dims[axis_at] // parts).reshape([-1 if axis == axis_at else 1 for axis in range(len(dims))])
    return gain


def noise(own_key, dims, spread, most, pieces=(), kind=jnp.bfloat16):
    gain = levels(own_key, dims, pieces, -0.22, 0.18) if pieces else 1.0
    array = jax.random.normal(own_key, dims, jnp.float32) * spread * gain
    return jnp.minimum(jnp.maximum(array, -most), most).astype(kind)


def setup_inputs(seed: int = 0) -> dict:
    keys = jax.random.split(jax.random.key(seed), 6)
    return {
        "features": noise(keys[0], (SAMPLES, C, NX, NY, NZ), 1.0, 6.0, ((0, 16), (2, 32))),
        "cotangent": noise(keys[1], (SAMPLES, C, NX, NY, NZ), 1.0, 6.0, ((0, 16), (2, 32))),
        "spectral": noise(keys[2], (KY * KZ, KX, 2 * C * C), (max(1, 8 * KX * KY * KZ * C // (NX * NY * NZ))) ** -0.5, 3.0, ((0, 32), (1, 16))),
        "pointwise": noise(keys[3], (C, C), C ** -0.5, 1.0),
        "biases": noise(keys[4], (C,), 0.5, 3.0),
    }


tanh_coef = 0.7978845608028654
cubic_coef = 0.044715

def frequencies(kept_count, length):
    indices = jnp.arange(kept_count, dtype=jnp.int32)
    return jnp.where(indices < kept_count // 2, indices, indices + (length - kept_count))

def plane_table(count_y, count_z, kept_y, kept_z):
    freq_y = frequencies(kept_y, count_y)
    freq_z = jnp.arange(kept_z, dtype=jnp.int32)
    turn_y = jnp.arange(count_y, dtype=jnp.int32)[:, None] * freq_y[None, :] % count_y
    turn_z = jnp.arange(count_z, dtype=jnp.int32)[:, None] * freq_z[None, :] % count_z
    angles = 2.0 * math.pi * (turn_y[:, None, :, None].astype(jnp.float32) / count_y + turn_z[None, :, None, :].astype(jnp.float32) / count_z)
    factor = 1.0 / math.sqrt(count_y * count_z)
    basis_table = jnp.stack([factor * jnp.cos(angles), -factor * jnp.sin(angles)], axis=-1)
    return basis_table.reshape(count_y * count_z, kept_y * kept_z, 2).astype(jnp.bfloat16)

def line_table(full_length, kept_count):
    freq_x = frequencies(kept_count, full_length)
    turns = jnp.arange(full_length, dtype=jnp.int32)[:, None] * freq_x[None, :] % full_length
    angles = 2.0 * math.pi * turns.astype(jnp.float32) / full_length
    factor = 1.0 / math.sqrt(full_length)
    cos_part = factor * jnp.cos(angles)
    sine_part = factor * jnp.sin(angles)
    first_row = jnp.stack([cos_part, -sine_part], axis=1)
    second = jnp.stack([sine_part, cos_part], axis=1)
    return jnp.stack([first_row, second], axis=0).astype(jnp.bfloat16)

def mode_doubling(kept_y, kept_z):
    mode_index = jnp.arange(kept_y * kept_z, dtype=jnp.int32) % kept_z
    return jnp.where(mode_index == 0, 1.0, 2.0).astype(jnp.float32)

def gelu_slope(values):
    inner_arg = tanh_coef * (values + cubic_coef * values * values * values)
    tanh_part = jnp.tanh(inner_arg)
    return 0.5 * (1.0 + tanh_part) + 0.5 * values * (1.0 - tanh_part * tanh_part) * tanh_coef * (1.0 + 3.0 * cubic_coef * values * values)

def product(equation, left_op, right_op):
    return jnp.einsum(equation, left_op.astype(jnp.float32), right_op.astype(jnp.float32))

def forward_lines(coarse, line_basis):
    return product('xpscm,pxqk->kqscm', coarse, line_basis).astype(jnp.bfloat16)

def inverse_lines(spectrum, line_basis):
    return product('kqscm,pxqk->xpscm', spectrum, line_basis).astype(jnp.bfloat16)

def spectral_mix(spectrum, weights):
    real_part = spectrum[:, 0]
    imag_part = spectrum[:, 1]
    w_real = weights[:, :, 0]
    w_imag = weights[:, :, 1]
    out_real = product('ksim,mkio->ksom', real_part, w_real) - product('ksim,mkio->ksom', imag_part, w_imag)
    out_imag = product('ksim,mkio->ksom', real_part, w_imag) + product('ksim,mkio->ksom', imag_part, w_real)
    return jnp.stack([out_real, out_imag], axis=1).astype(jnp.bfloat16)

def spectral_pull(adjoint, weights):
    real_part = adjoint[:, 0]
    imag_part = adjoint[:, 1]
    w_real = weights[:, :, 0]
    w_imag = weights[:, :, 1]
    out_real = product('ksom,mkio->ksim', real_part, w_real) + product('ksom,mkio->ksim', imag_part, w_imag)
    out_imag = product('ksom,mkio->ksim', imag_part, w_real) - product('ksom,mkio->ksim', real_part, w_imag)
    return jnp.stack([out_real, out_imag], axis=1).astype(jnp.bfloat16)

def weight_grad(spectrum, adjoint):
    spec_real = spectrum[:, 0]
    spec_imag = spectrum[:, 1]
    adj_real = adjoint[:, 0]
    adj_imag = adjoint[:, 1]
    grad_real = product('ksim,ksom->mkio', spec_real, adj_real) + product('ksim,ksom->mkio', spec_imag, adj_imag)
    grad_imag = product('ksim,ksom->mkio', spec_real, adj_imag) - product('ksim,ksom->mkio', spec_imag, adj_real)
    return jnp.stack([grad_real, grad_imag], axis=2)

def reference(features, cotangent, spectral, pointwise, biases):
    full_length = features.shape[2]
    plane_basis = plane_table(NY, NZ, KY, KZ)
    line_basis = line_table(full_length, KX)
    doubling = mode_doubling(KY, KZ)
    weights = spectral.reshape(KY * KZ, KX, 2, C, C)

    def one_sample(running, sample_pair):
        sample_in, sample_grad = sample_pair
        flat_cells = sample_in.reshape(1, C, full_length, NY * NZ)
        coarse = product('scxq,qmp->xpscm', flat_cells, plane_basis).astype(jnp.bfloat16)
        spectrum = forward_lines(coarse, line_basis)
        mixed_modes = spectral_mix(spectrum, weights)
        returned = inverse_lines(mixed_modes, line_basis)
        scaled = returned.astype(jnp.float32) * doubling[None, None, None, None, :]
        spectral_part = product('xpscm,qmp->scxq', scaled, plane_basis)
        linear = product('sicq,io->socq', flat_cells, pointwise)
        pre_act = linear + biases.astype(jnp.float32)[None, :, None, None] + spectral_part
        upstream_grad = sample_grad.reshape(1, C, full_length, NY * NZ).astype(jnp.float32)
        delta_cells = (upstream_grad * gelu_slope(pre_act)).astype(jnp.bfloat16)
        coarse_back = (product('scxq,qmp->xpscm', delta_cells, plane_basis) * doubling[None, None, None, None, :]).astype(jnp.bfloat16)
        adjoint = forward_lines(coarse_back, line_basis)
        pulled = spectral_pull(adjoint, weights)
        grad_terms = weight_grad(spectrum, adjoint)
        back_cells = inverse_lines(pulled, line_basis)
        grad_cells = product('socq,io->sicq', delta_cells, pointwise) + product('xpscm,qmp->scxq', back_cells, plane_basis)
        return (running + grad_terms, grad_cells.astype(jnp.bfloat16).reshape(C, full_length, NY, NZ))
    start_sum = jnp.zeros((KY * KZ, KX, 2, C, C), jnp.float32)
    running, grad_input = lax.scan(one_sample, start_sum, (features, cotangent))
    return (grad_input, running.reshape(KY * KZ, KX, 2 * C * C))
```

```python
import math

import numpy as np
import jax
import jax.numpy as jnp
from jax import lax
from jax.experimental import pallas as pl
from jax.experimental.pallas import tpu as pltpu
from jax.sharding import PartitionSpec as P

KX = 32
KY = 32
KZ = 8
NY = 32
NZ = 128
NX = 128
C = 32
SLAB = 4
STEPS = 15

tanh_coef = 0.7978845608028654
cubic_coef = 0.044715

F32 = jnp.float32
BF16 = jnp.bfloat16


def frequencies(kept_count, length):
    indices = np.arange(kept_count, dtype=np.int32)
    return np.where(indices < kept_count // 2, indices, indices + (length - kept_count)).astype(np.int32)


def plane_table():
    freq_y = frequencies(KY, NY)
    freq_z = np.arange(KZ, dtype=np.int32)
    ys = np.array(list(range(1, 16)) + [0, 16], dtype=np.int32)
    turn_y = ys[:, None] * freq_y[None, :] % NY
    turn_z = np.arange(NZ, dtype=np.int32)[:, None] * freq_z[None, :] % NZ
    angles = np.float32(2.0 * math.pi) * (
        turn_y[:, None, :, None].astype(np.float32) / np.float32(NY)
        + turn_z[None, :, None, :].astype(np.float32) / np.float32(NZ)
    )
    factor = np.float32(1.0 / math.sqrt(NY * NZ))
    table = np.stack([factor * np.cos(angles), -factor * np.sin(angles)], axis=-1)
    table = table.reshape(17, NZ, KY, 2, 4, 2).transpose(2, 4, 3, 5, 0, 1)
    return table.reshape(KY * KZ * 2, 17 * NZ).astype(BF16)


def line_table():
    freq_x = frequencies(KX, NX)
    turns = np.arange(NX, dtype=np.int32)[:, None] * freq_x[None, :] % NX
    angles = np.float32(2.0 * math.pi) * turns.astype(np.float32) / np.float32(NX)
    factor = np.float32(1.0 / math.sqrt(NX))
    cos_part = factor * np.cos(angles)
    sine_part = factor * np.sin(angles)
    first_row = np.stack([cos_part, -sine_part], axis=1)
    second = np.stack([sine_part, cos_part], axis=1)
    line = np.stack([first_row, second], axis=0)
    line = line.reshape(2, 32, 4, 2, 16, 2).transpose(4, 3, 5, 1, 2, 0)
    full = np.zeros((16, 2, 2, 2, 32, 4, 2, 2), np.float32)
    for hi in range(2):
        full[:, :, hi, :, :, :, hi, :] = line
    return full.reshape(128, 512).astype(BF16)


def gelu_slope(values):
    inner_arg = tanh_coef * (values + cubic_coef * values * values * values)
    tanh_part = jnp.tanh(inner_arg)
    return 0.5 * (1.0 + tanh_part) + 0.5 * values * (1.0 - tanh_part * tanh_part) * tanh_coef * (
        1.0 + 3.0 * cubic_coef * values * values
    )


def dot(left, right, dims=((1,), (0,))):
    return lax.dot_general(left, right, (dims, ((), ())), preferred_element_type=F32)


def iota(shape, axis):
    return lax.broadcasted_iota(jnp.int32, shape, axis)


def as_bf16(condition):
    return jnp.where(condition, 1.0, 0.0).astype(BF16)


def swap_blocks(value):
    v = value.reshape(64, 8, 128)
    row_low = iota((1, 8, 128), 1) >> 2
    lane = iota((1, 8, 128), 2) >> 5
    lane_low = lane & 1
    lane_high = lane >> 1
    turned = pltpu.roll(v, 4, 1)
    up = pltpu.roll(turned, 32, 2)
    down = pltpu.roll(turned, 96, 2)
    v = jnp.where(row_low == lane_low, v, jnp.where(lane_low == 1, up, down))
    v = v.reshape(32, 2, 8, 128)
    first, second = v[:, 0], v[:, 1]
    new_first = jnp.where(lane_high == 0, first, pltpu.roll(second, 64, 2))
    new_second = jnp.where(lane_high == 1, second, pltpu.roll(first, 64, 2))
    return jnp.stack([new_first, new_second], axis=1).reshape(512, 128)


def negate_jy(value):
    return jnp.concatenate([value[16 * ((32 - j) % 32) : 16 * ((32 - j) % 32) + 16] for j in range(32)], axis=0)


def doubled(value):
    jz = iota(value.shape, 0) & 14
    return value * jnp.where(jz == 0, 1.0, 2.0)


def gather_rows(wide, y):
    return jnp.concatenate(
        [wide[pl.ds(x * NY + y, C, stride=SLAB * NY), :] for x in range(SLAB)], axis=0
    )


def regroup(source_ref, wide, pairs_ref):
    wide[...] = source_ref[...].astype(F32)
    for s in range(1, 17):
        lanes = pl.ds((s - 1) * NZ, NZ)
        above, below = (0, 16) if s == 16 else (s, NY - s)
        pairs_ref[0:128, lanes] = gather_rows(wide, above).astype(BF16)
        pairs_ref[128:256, lanes] = gather_rows(wide, below).astype(BF16)


def to_coarse(table_ref, pairs_ref):
    last = slice(STEPS * NZ, 16 * NZ)
    both = dot(table_ref[:, 0 : STEPS * NZ], pairs_ref[:, 0 : STEPS * NZ], ((1,), (1,)))
    alone = dot(table_ref[:, last], pairs_ref[0:128, last], ((1,), (1,)))
    alone = alone + dot(table_ref[:, 16 * NZ : 17 * NZ], pairs_ref[128:256, last], ((1,), (1,)))
    return alone + both[:, 0:128] + negate_jy(both[:, 128:256])


def analyse_kernel(features_ref, table_ref, send_ref, pairs_out, wide, pairs_ref, sem):
    regroup(features_ref, wide, pairs_ref)
    copy = pltpu.make_async_copy(pairs_ref, pairs_out, sem)
    copy.start()
    coarse = to_coarse(table_ref, pairs_ref)
    send_ref[...] = swap_blocks(coarse).astype(BF16).reshape(32, 16, 128)
    copy.wait()


def regroup_kernel(source_ref, pairs_out, wide, pairs_ref, sem):
    regroup(source_ref, wide, pairs_ref)
    copy = pltpu.make_async_copy(pairs_ref, pairs_out, sem)
    copy.start()
    copy.wait()


def block_of(row):
    return ((row >> 7) & 1) * 8 + ((row >> 4) & 3) * 2 + ((row >> 6) & 1)


def repeat_kernel(spectral_ref, out_ref):
    rows = jnp.concatenate([spectral_ref[m].astype(F32) for m in range(8)], axis=0).astype(BF16)
    for z in range(8):
        out_ref[z] = rows


def weight_columns(low_ref, high_ref, start):
    lanes = slice(start, start + 128)
    return jnp.concatenate([low_ref[:, lanes], high_ref[:, lanes]], axis=0).astype(F32)


def spread_rows(compact):
    row = iota((512, 128), 0)
    wanted = block_of(row) * 8 + (row >> 8) * 4 + ((row >> 3) & 1) * 2 + (row & 1)
    select = as_bf16(wanted == iota((512, 128), 1))
    rows = dot(select, compact)
    return jnp.where((iota((512, 128), 1) >> 5) == ((row >> 1) & 3), rows, 0.0).astype(BF16)


def close_rows(rows):
    row = iota((512, 128), 0)
    kept = jnp.where((iota((512, 128), 1) >> 5) == ((row >> 1) & 3), rows, 0.0).astype(BF16)
    col = iota((128, 512), 1)
    wanted = block_of(col) * 8 + (col >> 8) * 4 + ((col >> 3) & 1) * 2 + (col & 1)
    select = as_bf16(wanted == iota((128, 512), 0))
    return dot(select, kept).astype(BF16)


def mix_kernel(recv_ref, low_ref, high_ref, line_ref, send_out, spec_out, send_ref, spec_ref, sems):
    compact = dot(line_ref[...], recv_ref[...].reshape(512, 128)).astype(BF16)
    spec_ref[...] = compact.astype(F32)
    spec_copy = pltpu.make_async_copy(spec_ref, spec_out, sems.at[0])
    spec_copy.start()
    rows = spread_rows(compact)
    out_real = jnp.zeros((256, 128), F32)
    out_imag = jnp.zeros((256, 128), F32)
    for t in range(8):
        spread = as_bf16((iota((128, 128), 0) & 31) == t * 4 + (iota((128, 128), 1) >> 5))
        wide = dot(rows, spread)
        s_real, s_imag = wide[0:256], wide[256:512]
        w_real = weight_columns(low_ref, high_ref, t * 128)
        w_imag = weight_columns(low_ref, high_ref, 1024 + t * 128)
        out_real = out_real + (s_real * w_real - s_imag * w_imag)
        out_imag = out_imag + (s_real * w_imag + s_imag * w_real)
    mixed = jnp.concatenate([out_real, out_imag], axis=0)
    mixed = mixed + pltpu.roll(mixed, 32, 1)
    mixed = mixed + pltpu.roll(mixed, 64, 1)
    compact = close_rows(mixed)
    send_ref[...] = dot(line_ref[...], compact, ((0,), (0,))).astype(BF16).reshape(32, 16, 128)
    send_copy = pltpu.make_async_copy(send_ref, send_out, sems.at[1])
    send_copy.start()
    spec_copy.wait()
    send_copy.wait()


def pull_kernel(recv_ref, low_ref, high_ref, line_ref, spec_ref, send_ref, pair_ref):
    compact = dot(line_ref[...], recv_ref[...].reshape(512, 128)).astype(BF16)
    pair_ref[...] = jnp.concatenate(
        [spec_ref[...].reshape(16, 8, 128), compact.astype(F32).reshape(16, 8, 128)], axis=1
    ).astype(BF16)
    rows = spread_rows(compact)
    repeat = as_bf16((iota((128, 128), 0) & 31) == (iota((128, 128), 1) & 31))
    wide = dot(rows, repeat)
    a_real, a_imag = wide[0:256], wide[256:512]
    pulled = jnp.zeros((512, 128), F32)
    for t in range(4):
        parts = []
        for u in range(2):
            w_real = weight_columns(low_ref, high_ref, (2 * t + u) * 128)
            w_imag = weight_columns(low_ref, high_ref, 1024 + (2 * t + u) * 128)
            parts.append(
                jnp.concatenate(
                    [a_real * w_real + a_imag * w_imag, a_imag * w_real - a_real * w_imag], axis=0
                ).astype(BF16)
            )
        collect = as_bf16((iota((256, 128), 0) >> 5) + t * 8 == (iota((256, 128), 1) & 31))
        pulled = pulled + dot(jnp.concatenate(parts, axis=1), collect)
    compact = close_rows(pulled)
    send_ref[...] = dot(line_ref[...], compact, ((0,), (0,))).astype(BF16).reshape(32, 16, 128)


def block_weights(weights_ref, transposed):
    spread = as_bf16((iota((256, 32), 0) & 31) == iota((256, 32), 1))
    dims = ((1,), (1,)) if transposed else ((1,), (0,))
    tall = dot(spread, weights_ref[...], dims).astype(BF16)
    full = dot(tall, spread, ((1,), (1,)))
    same = (iota((256, 256), 0) >> 5) == (iota((256, 256), 1) >> 5)
    return jnp.where(same, full, 0.0).astype(BF16), spread


def profiles(recv_ref, scale):
    value = swap_blocks(recv_ref[...].astype(F32).reshape(512, 128))
    if scale:
        value = doubled(value)
    both = jnp.concatenate([value, negate_jy(value)], axis=1)
    return both.T.astype(BF16)


def step_lanes():
    return [(2 * t * NZ, 2 * NZ) for t in range(7)] + [(14 * NZ, NZ)]


def nonlinear_kernel(
    recv_ref, table_ref, x_hbm, c_hbm, weights_ref, bias_ref, send_ref, delta_out, x_ref, c_ref, delta_ref, sems
):
    x_copy = pltpu.make_async_copy(x_hbm, x_ref, sems.at[0])
    x_copy.start()
    c_copy = pltpu.make_async_copy(c_hbm, c_ref, sems.at[1])
    c_copy.start()
    basis = profiles(recv_ref, True)
    mixing, spread = block_weights(weights_ref, True)
    bias = dot(spread, bias_ref[...])
    x_copy.wait()
    c_copy.wait()
    for start, width in step_lanes():
        lanes = slice(start, start + width)
        pre = dot(basis, table_ref[:, lanes]) + dot(mixing, x_ref[:, lanes]) + bias[:, 0:width]
        delta_ref[:, lanes] = (c_ref[:, lanes].astype(F32) * gelu_slope(pre)).astype(BF16)
    last = slice(STEPS * NZ, 16 * NZ)
    alone = jnp.concatenate(
        [dot(basis[0:128], table_ref[:, last]), dot(basis[0:128], table_ref[:, 16 * NZ : 17 * NZ])], axis=0
    )
    pre = alone + dot(mixing, x_ref[:, last]) + bias[:, 0:NZ]
    delta_ref[:, last] = (c_ref[:, last].astype(F32) * gelu_slope(pre)).astype(BF16)
    copy = pltpu.make_async_copy(delta_ref, delta_out, sems.at[2])
    copy.start()
    coarse = doubled(to_coarse(table_ref, delta_ref))
    send_ref[...] = swap_blocks(coarse).astype(BF16).reshape(32, 16, 128)
    copy.wait()


def input_grad_kernel(recv_ref, table_ref, delta_hbm, weights_ref, out_ref, wide, delta_ref, sem):
    copy = pltpu.make_async_copy(delta_hbm, delta_ref, sem)
    copy.start()
    basis = profiles(recv_ref, False)
    mixing, _ = block_weights(weights_ref, False)
    copy.wait()

    def put(value, y):
        for x in range(SLAB):
            wide[pl.ds(x * NY + y, C, stride=SLAB * NY), :] = value[x * C : x * C + C]

    for start, width in step_lanes():
        lanes = slice(start, start + width)
        grad = dot(basis, table_ref[:, lanes]) + dot(mixing, delta_ref[:, lanes])
        for u in range(width // NZ):
            s = start // NZ + u + 1
            put(grad[0:128, u * NZ : u * NZ + NZ], s)
            put(grad[128:256, u * NZ : u * NZ + NZ], NY - s)
    last = slice(STEPS * NZ, 16 * NZ)
    linear = dot(mixing, delta_ref[:, last])
    put(dot(basis[0:128], table_ref[:, last]) + linear[0:128], 0)
    put(dot(basis[0:128], table_ref[:, 16 * NZ : 17 * NZ]) + linear[128:256], 16)
    out_ref[...] = wide[...].astype(BF16)


def weight_grad_kernel(pair_ref, out_ref):
    row = iota((1024, 256), 0)
    wanted = ((row >> 4) & 15) * 16 + (row >> 9) * 8 + ((row >> 8) & 1) * 4 + ((row >> 3) & 1) * 2 + (row & 1)
    select = as_bf16(wanted == iota((1024, 256), 1))
    rows = dot(select, pair_ref[...].reshape(256, 128))
    row = iota((1024, 128), 0)
    rows = jnp.where((iota((1024, 128), 1) >> 5) == ((row >> 1) & 3), rows, 0.0).astype(BF16)
    repeat = as_bf16((iota((128, 128), 0) & 31) == (iota((128, 128), 1) & 31))
    wide = dot(rows[512:1024], repeat)
    a_real, a_imag = wide[0:256], wide[256:512]
    for t in range(8):
        spread = as_bf16((iota((128, 128), 0) & 31) == t * 4 + (iota((128, 128), 1) >> 5))
        wide = dot(rows[0:512], spread)
        s_real, s_imag = wide[0:256], wide[256:512]
        grad_real = jnp.sum((s_real * a_real + s_imag * a_imag).reshape(16, 16, 128), axis=0)
        grad_imag = jnp.sum((s_real * a_imag - s_imag * a_real).reshape(16, 16, 128), axis=0)
        for m in range(8):
            out_ref[m, :, t * 128 : t * 128 + 128] = grad_real[2 * m : 2 * m + 2]
            out_ref[m, :, 1024 + t * 128 : 1024 + t * 128 + 128] = grad_imag[2 * m : 2 * m + 2]


def run(kernel, name, outs, args, flops, scratch=(), out_hbm=(), in_hbm=()):
    args = [pltpu.with_memory_space_constraint(a, pltpu.HBM) if k in in_hbm else a for k, a in enumerate(args)]
    shapes = [(pltpu.HBM if k in out_hbm else jax.ShapeDtypeStruct)(*out) for k, out in enumerate(outs)]
    return pl.pallas_call(
        kernel,
        out_shape=shapes,
        in_specs=[
            pl.BlockSpec(memory_space=pltpu.HBM if k in in_hbm else pltpu.VMEM) for k in range(len(args))
        ],
        out_specs=[
            pl.BlockSpec(memory_space=pltpu.HBM if k in out_hbm else pltpu.VMEM) for k in range(len(outs))
        ],
        scratch_shapes=list(scratch),
        compiler_params=pltpu.CompilerParams(vmem_limit_bytes=32 * 2**20),
        cost_estimate=pl.CostEstimate(flops=flops, bytes_accessed=2 * 2**20, transcendentals=0),
        name=name,
    )(*args)


def exchange(value, axis):
    return lax.all_to_all(value, axis, split_axis=0, concat_axis=0, tiled=True)


def body(features, cotangent, spectral, pointwise, biases):
    table = jnp.asarray(plane_table())
    line = jnp.asarray(line_table())
    piece = ((32, 16, 128), BF16)
    pairs = ((256, 16 * NZ), BF16)
    wide = pltpu.VMEM((C * SLAB * NY, NZ), F32)
    held = pltpu.VMEM(*pairs)
    sem = pltpu.SemaphoreType.DMA(())

    same_core = [[2 * z + core for z in range(8)] for core in range(2)]
    same_chip = [[2 * z, 2 * z + 1] for z in range(8)]
    (copies,) = run(repeat_kernel, "repeat", [((8, 16, 2048), BF16)], [spectral], 10**6)
    blocks = lax.all_to_all(copies, "dp", 0, 0, tiled=True, axis_index_groups=same_core)
    send, x_pairs = run(
        analyse_kernel, "analyse", [piece, pairs], [features.reshape(C * SLAB * NY, NZ), table], 10**9,
        [wide, held, sem], (1,),
    )
    send, blocks = lax.optimization_barrier((send, blocks))
    w_low, w_high = (
        lax.all_gather(blocks[4 * h : 4 * h + 4], "dp", axis=0, tiled=True, axis_index_groups=same_chip).reshape(128, 2048)
        for h in range(2)
    )
    (c_pairs,) = run(
        regroup_kernel, "regroup", [pairs], [cotangent.reshape(C * SLAB * NY, NZ)], 10**6, [wide, held, sem], (0,)
    )
    send, spec = run(
        mix_kernel, "mix", [piece, ((128, 128), F32)], [exchange(send, "space"), w_low, w_high, line], 10**8,
        [pltpu.VMEM(*piece), pltpu.VMEM((128, 128), F32), pltpu.SemaphoreType.DMA((2,))], (0, 1),
    )
    bias = jnp.broadcast_to(biases[:, None], (C, 2 * NZ))
    send, delta = run(
        nonlinear_kernel, "nonlinear", [piece, pairs],
        [exchange(send, "space"), table, x_pairs, c_pairs, pointwise, bias], 2 * 10**9,
        [held, held, held, pltpu.SemaphoreType.DMA((3,))], (1,), (2, 3),
    )
    send, pair = run(
        pull_kernel, "pull", [piece, ((16, 16, 128), BF16)],
        [exchange(send, "space"), w_low, w_high, line, spec], 10**8,
    )
    recv = exchange(send, "space")
    pair, recv = lax.optimization_barrier((pair, recv))
    pair = exchange(pair, "dp")
    (grad_input,) = run(
        input_grad_kernel, "input_grad", [((C * SLAB * NY, NZ), BF16)],
        [recv, table, delta, pointwise], 10**9, [wide, held, sem], (), (2,),
    )
    (grad_spectral,) = run(weight_grad_kernel, "weight_grad", [((8, 2, 2048), F32)], [pair], 10**8)
    return grad_input.reshape(features.shape), grad_spectral


def solution(mesh):
    placed = (
        P("dp", None, "space", None, None),
        P("dp", None, "space", None, None),
        P("space", "dp", None),
        P(),
        P(),
    )
    return jax.shard_map(
        body,
        mesh=mesh,
        in_specs=placed,
        out_specs=(P("dp", None, "space", None, None), P("space", "dp", None)),
        check_vma=False,
    )
```

```python
import math

import numpy as np
import jax
import jax.numpy as jnp
from jax import lax
from jax.experimental import pallas as pl
from jax.experimental.pallas import tpu as pltpu
from jax.sharding import PartitionSpec as P

KX = 32
KY = 32
KZ = 8
NY = 32
NZ = 128
NX = 128
C = 32
SLAB = 4
STEPS = 15

tanh_coef = 0.7978845608028654
cubic_coef = 0.044715

F32 = jnp.float32
BF16 = jnp.bfloat16


def frequencies(kept_count, length):
    indices = np.arange(kept_count, dtype=np.int32)
    return np.where(indices < kept_count // 2, indices, indices + (length - kept_count)).astype(np.int32)


def plane_table():
    freq_y = frequencies(KY, NY)
    freq_z = np.arange(KZ, dtype=np.int32)
    ys = np.array(list(range(1, 16)) + [0, 16], dtype=np.int32)
    turn_y = ys[:, None] * freq_y[None, :] % NY
    turn_z = np.arange(NZ, dtype=np.int32)[:, None] * freq_z[None, :] % NZ
    angles = np.float32(2.0 * math.pi) * (
        turn_y[:, None, :, None].astype(np.float32) / np.float32(NY)
        + turn_z[None, :, None, :].astype(np.float32) / np.float32(NZ)
    )
    factor = np.float32(1.0 / math.sqrt(NY * NZ))
    table = np.stack([factor * np.cos(angles), -factor * np.sin(angles)], axis=-1)
    table = table.reshape(17, NZ, KY, 2, 4, 2).transpose(2, 4, 3, 5, 0, 1)
    return table.reshape(KY * KZ * 2, 17 * NZ).astype(BF16)


def line_table():
    freq_x = frequencies(KX, NX)
    turns = np.arange(NX, dtype=np.int32)[:, None] * freq_x[None, :] % NX
    angles = np.float32(2.0 * math.pi) * turns.astype(np.float32) / np.float32(NX)
    factor = np.float32(1.0 / math.sqrt(NX))
    cos_part = factor * np.cos(angles)
    sine_part = factor * np.sin(angles)
    first_row = np.stack([cos_part, -sine_part], axis=1)
    second = np.stack([sine_part, cos_part], axis=1)
    line = np.stack([first_row, second], axis=0)
    line = line.reshape(2, 32, 4, 2, 16, 2).transpose(4, 3, 5, 1, 2, 0)
    full = np.zeros((16, 2, 2, 2, 32, 4, 2, 2), np.float32)
    for hi in range(2):
        full[:, :, hi, :, :, :, hi, :] = line
    return full.reshape(128, 512).astype(BF16)


def gelu_slope(values):
    square = values * values
    half = 0.5 + 0.5 * jnp.tanh(values * (tanh_coef + (tanh_coef * cubic_coef) * square))
    return half + (half - half * half) * (values * (2.0 * tanh_coef + (6.0 * tanh_coef * cubic_coef) * square))


def dot(left, right, dims=((1,), (0,))):
    return lax.dot_general(left, right, (dims, ((), ())), preferred_element_type=F32)


def iota(shape, axis):
    return lax.broadcasted_iota(jnp.int32, shape, axis)


def as_bf16(condition):
    return jnp.where(condition, 1.0, 0.0).astype(BF16)


def swap_blocks(value):
    v = value.reshape(64, 8, 128)
    row_low = iota((1, 8, 128), 1) >> 2
    lane = iota((1, 8, 128), 2) >> 5
    lane_low = lane & 1
    lane_high = lane >> 1
    turned = pltpu.roll(v, 4, 1)
    up = pltpu.roll(turned, 32, 2)
    down = pltpu.roll(turned, 96, 2)
    v = jnp.where(row_low == lane_low, v, jnp.where(lane_low == 1, up, down))
    v = v.reshape(32, 2, 8, 128)
    first, second = v[:, 0], v[:, 1]
    new_first = jnp.where(lane_high == 0, first, pltpu.roll(second, 64, 2))
    new_second = jnp.where(lane_high == 1, second, pltpu.roll(first, 64, 2))
    return jnp.stack([new_first, new_second], axis=1).reshape(512, 128)


def negate_jy(value):
    return jnp.concatenate([value[16 * ((32 - j) % 32) : 16 * ((32 - j) % 32) + 16] for j in range(32)], axis=0)


def doubled(value):
    jz = iota(value.shape, 0) & 14
    return value * jnp.where(jz == 0, 1.0, 2.0)


def gather_rows(wide, y):
    return jnp.concatenate(
        [wide[pl.ds(x * NY + y, C, stride=SLAB * NY), :] for x in range(SLAB)], axis=0
    )


def regroup(source_ref, wide, pairs_ref):
    wide[...] = source_ref[...].astype(F32)
    for s in range(1, 17):
        lanes = pl.ds((s - 1) * NZ, NZ)
        above, below = (0, 16) if s == 16 else (s, NY - s)
        pairs_ref[0:128, lanes] = gather_rows(wide, above).astype(BF16)
        pairs_ref[128:256, lanes] = gather_rows(wide, below).astype(BF16)


def to_coarse(table_ref, pairs_ref):
    last = slice(STEPS * NZ, 16 * NZ)
    both = dot(table_ref[:, 0 : STEPS * NZ], pairs_ref[:, 0 : STEPS * NZ], ((1,), (1,)))
    alone = dot(table_ref[:, last], pairs_ref[0:128, last], ((1,), (1,)))
    alone = alone + dot(table_ref[:, 16 * NZ : 17 * NZ], pairs_ref[128:256, last], ((1,), (1,)))
    return alone + both[:, 0:128] + negate_jy(both[:, 128:256])


def analyse_kernel(features_ref, table_ref, send_ref, pairs_out, wide, pairs_ref, sem):
    regroup(features_ref, wide, pairs_ref)
    copy = pltpu.make_async_copy(pairs_ref, pairs_out, sem)
    copy.start()
    coarse = to_coarse(table_ref, pairs_ref)
    send_ref[...] = swap_blocks(coarse).astype(BF16).reshape(32, 16, 128)
    copy.wait()


def regroup_kernel(source_ref, pairs_out, wide, pairs_ref, sem):
    regroup(source_ref, wide, pairs_ref)
    copy = pltpu.make_async_copy(pairs_ref, pairs_out, sem)
    copy.start()
    copy.wait()


def block_of(row):
    return ((row >> 7) & 1) * 8 + ((row >> 4) & 3) * 2 + ((row >> 6) & 1)


def repeat_kernel(spectral_ref, out_hbm, rows_ref, sems):
    rows_ref[...] = jnp.concatenate([spectral_ref[m].astype(F32) for m in range(8)], axis=0).astype(BF16)
    copies = [pltpu.make_async_copy(rows_ref, out_hbm.at[z], sems.at[z]) for z in range(8)]
    for copy in copies:
        copy.start()
    for copy in copies:
        copy.wait()


def weight_columns(low_ref, high_ref, start):
    lanes = slice(start, start + 128)
    return jnp.concatenate([low_ref[:, lanes], high_ref[:, lanes]], axis=0).astype(F32)


def spread_rows(compact):
    row = iota((512, 128), 0)
    wanted = block_of(row) * 8 + (row >> 8) * 4 + ((row >> 3) & 1) * 2 + (row & 1)
    select = as_bf16(wanted == iota((512, 128), 1))
    rows = dot(select, compact)
    return jnp.where((iota((512, 128), 1) >> 5) == ((row >> 1) & 3), rows, 0.0).astype(BF16)


def close_rows(rows):
    row = iota((512, 128), 0)
    kept = jnp.where((iota((512, 128), 1) >> 5) == ((row >> 1) & 3), rows, 0.0).astype(BF16)
    col = iota((128, 512), 1)
    wanted = block_of(col) * 8 + (col >> 8) * 4 + ((col >> 3) & 1) * 2 + (col & 1)
    select = as_bf16(wanted == iota((128, 512), 0))
    return dot(select, kept).astype(BF16)


def mix_kernel(recv_ref, low_ref, high_ref, line_ref, send_ref, spec_out, spec_ref, sem):
    compact = dot(line_ref[...], recv_ref[...].reshape(512, 128)).astype(BF16)
    spec_ref[...] = compact.astype(F32)
    spec_copy = pltpu.make_async_copy(spec_ref, spec_out, sem)
    spec_copy.start()
    rows = spread_rows(compact)
    out_real = jnp.zeros((256, 128), F32)
    out_imag = jnp.zeros((256, 128), F32)
    for t in range(8):
        spread = as_bf16((iota((128, 128), 0) & 31) == t * 4 + (iota((128, 128), 1) >> 5))
        wide = dot(rows, spread)
        s_real, s_imag = wide[0:256], wide[256:512]
        w_real = weight_columns(low_ref, high_ref, t * 128)
        w_imag = weight_columns(low_ref, high_ref, 1024 + t * 128)
        out_real = out_real + (s_real * w_real - s_imag * w_imag)
        out_imag = out_imag + (s_real * w_imag + s_imag * w_real)
    mixed = jnp.concatenate([out_real, out_imag], axis=0)
    mixed = mixed + pltpu.roll(mixed, 32, 1)
    mixed = mixed + pltpu.roll(mixed, 64, 1)
    compact = close_rows(mixed)
    send_ref[...] = dot(line_ref[...], compact, ((0,), (0,))).astype(BF16).reshape(32, 16, 128)
    spec_copy.wait()


def pull_kernel(recv_ref, low_ref, high_ref, line_ref, spec_ref, send_ref, pair_ref):
    compact = dot(line_ref[...], recv_ref[...].reshape(512, 128)).astype(BF16)
    pair_ref[...] = jnp.concatenate(
        [spec_ref[...].reshape(16, 8, 128), compact.astype(F32).reshape(16, 8, 128)], axis=1
    ).astype(BF16)
    rows = spread_rows(compact)
    repeat = as_bf16((iota((128, 128), 0) & 31) == (iota((128, 128), 1) & 31))
    wide = dot(rows, repeat)
    a_real, a_imag = wide[0:256], wide[256:512]
    pulled = jnp.zeros((512, 128), F32)
    for t in range(4):
        parts = []
        for u in range(2):
            w_real = weight_columns(low_ref, high_ref, (2 * t + u) * 128)
            w_imag = weight_columns(low_ref, high_ref, 1024 + (2 * t + u) * 128)
            parts.append(
                jnp.concatenate(
                    [a_real * w_real + a_imag * w_imag, a_imag * w_real - a_real * w_imag], axis=0
                ).astype(BF16)
            )
        collect = as_bf16((iota((256, 128), 0) >> 5) + t * 8 == (iota((256, 128), 1) & 31))
        pulled = pulled + dot(jnp.concatenate(parts, axis=1), collect)
    compact = close_rows(pulled)
    send_ref[...] = dot(line_ref[...], compact, ((0,), (0,))).astype(BF16).reshape(32, 16, 128)


def block_weights(weights_ref, transposed):
    spread = as_bf16((iota((256, 32), 0) & 31) == iota((256, 32), 1))
    dims = ((1,), (1,)) if transposed else ((1,), (0,))
    tall = dot(spread, weights_ref[...], dims).astype(BF16)
    full = dot(tall, spread, ((1,), (1,)))
    same = (iota((256, 256), 0) >> 5) == (iota((256, 256), 1) >> 5)
    return jnp.where(same, full, 0.0).astype(BF16), spread


def profiles(recv_ref, scale):
    value = swap_blocks(recv_ref[...].astype(F32).reshape(512, 128))
    if scale:
        value = doubled(value)
    both = jnp.concatenate([value, negate_jy(value)], axis=1)
    return both.T.astype(BF16)


def quarters(source, target, sems):
    width = 4 * NZ
    return [
        pltpu.make_async_copy(
            source.at[:, pl.ds(q * width, width)], target.at[:, pl.ds(q * width, width)], sems.at[q]
        )
        for q in range(4)
    ]


def step_lanes():
    return [(2 * t * NZ, 2 * NZ) for t in range(7)] + [(14 * NZ, NZ)]


def nonlinear_kernel(
    recv_ref, table_ref, x_hbm, c_hbm, weights_ref, bias_ref, send_ref, delta_out, x_ref, c_ref, delta_ref, spec_ref, sems
):
    x_copies = quarters(x_hbm, x_ref, sems.at[0])
    c_copies = quarters(c_hbm, c_ref, sems.at[1])
    out_copies = quarters(delta_ref, delta_out, sems.at[2])
    for q in range(4):
        x_copies[q].start()
        c_copies[q].start()
    basis = profiles(recv_ref, True)
    mixing, spread = block_weights(weights_ref, True)
    bias = dot(spread, bias_ref[...])
    last = slice(STEPS * NZ, 16 * NZ)
    for start, width in step_lanes():
        lanes = slice(start, start + width)
        spec_ref[:, lanes] = dot(basis, table_ref[:, lanes]) + bias[:, 0:width]
    spec_ref[0:128, last] = dot(basis[0:128], table_ref[:, last]) + bias[0:128, 0:NZ]
    spec_ref[128:256, last] = dot(basis[0:128], table_ref[:, 16 * NZ : 17 * NZ]) + bias[128:256, 0:NZ]
    for q in range(4):
        x_copies[q].wait()
        c_copies[q].wait()
        for t in range(2):
            lanes = pl.ds((4 * q + 2 * t) * NZ, 2 * NZ)
            pre = spec_ref[:, lanes] + dot(mixing, x_ref[:, lanes])
            delta_ref[:, lanes] = (c_ref[:, lanes].astype(F32) * gelu_slope(pre)).astype(BF16)
        out_copies[q].start()
    coarse = doubled(to_coarse(table_ref, delta_ref))
    send_ref[...] = swap_blocks(coarse).astype(BF16).reshape(32, 16, 128)
    for copy in out_copies:
        copy.wait()


def input_grad_kernel(recv_ref, table_ref, delta_hbm, weights_ref, out_hbm, wide, delta_ref, out_ref, sems):
    copies = quarters(delta_hbm, delta_ref, sems.at[0])
    for copy in copies:
        copy.start()
    basis = profiles(recv_ref, False)
    mixing, _ = block_weights(weights_ref, False)

    def put(value, y):
        for x in range(SLAB):
            wide[pl.ds(x * NY + y, C, stride=SLAB * NY), :] = value[x * C : x * C + C]

    for t, (start, width) in enumerate(step_lanes()):
        if t % 2 == 0:
            copies[t // 2].wait()
        lanes = slice(start, start + width)
        grad = dot(basis, table_ref[:, lanes]) + dot(mixing, delta_ref[:, lanes])
        for u in range(width // NZ):
            s = start // NZ + u + 1
            put(grad[0:128, u * NZ : u * NZ + NZ], s)
            put(grad[128:256, u * NZ : u * NZ + NZ], NY - s)
    last = slice(STEPS * NZ, 16 * NZ)
    linear = dot(mixing, delta_ref[:, last])
    put(dot(basis[0:128], table_ref[:, last]) + linear[0:128], 0)
    put(dot(basis[0:128], table_ref[:, 16 * NZ : 17 * NZ]) + linear[128:256], 16)
    size = C * SLAB * NY // 4
    copies = []
    for q in range(4):
        rows = pl.ds(q * size, size)
        out_ref[rows, :] = wide[rows, :].astype(BF16)
        copies.append(pltpu.make_async_copy(out_ref.at[rows, :], out_hbm.at[rows, :], sems.at[1, q]))
        copies[q].start()
    for copy in copies:
        copy.wait()


def weight_grad_kernel(pair_ref, out_ref):
    row = iota((1024, 256), 0)
    wanted = ((row >> 4) & 15) * 16 + (row >> 9) * 8 + ((row >> 8) & 1) * 4 + ((row >> 3) & 1) * 2 + (row & 1)
    select = as_bf16(wanted == iota((1024, 256), 1))
    rows = dot(select, pair_ref[...].reshape(256, 128))
    row = iota((1024, 128), 0)
    rows = jnp.where((iota((1024, 128), 1) >> 5) == ((row >> 1) & 3), rows, 0.0).astype(BF16)
    repeat = as_bf16((iota((128, 128), 0) & 31) == (iota((128, 128), 1) & 31))
    wide = dot(rows[512:1024], repeat)
    a_real, a_imag = wide[0:256], wide[256:512]
    for t in range(8):
        spread = as_bf16((iota((128, 128), 0) & 31) == t * 4 + (iota((128, 128), 1) >> 5))
        wide = dot(rows[0:512], spread)
        s_real, s_imag = wide[0:256], wide[256:512]
        grad_real = jnp.sum((s_real * a_real + s_imag * a_imag).reshape(16, 16, 128), axis=0)
        grad_imag = jnp.sum((s_real * a_imag - s_imag * a_real).reshape(16, 16, 128), axis=0)
        for m in range(8):
            out_ref[m, :, t * 128 : t * 128 + 128] = grad_real[2 * m : 2 * m + 2]
            out_ref[m, :, 1024 + t * 128 : 1024 + t * 128 + 128] = grad_imag[2 * m : 2 * m + 2]


def run(kernel, name, outs, args, flops, scratch=(), out_hbm=(), in_hbm=()):
    args = [pltpu.with_memory_space_constraint(a, pltpu.HBM) if k in in_hbm else a for k, a in enumerate(args)]
    shapes = [(pltpu.HBM if k in out_hbm else jax.ShapeDtypeStruct)(*out) for k, out in enumerate(outs)]
    return pl.pallas_call(
        kernel,
        out_shape=shapes,
        in_specs=[
            pl.BlockSpec(memory_space=pltpu.HBM if k in in_hbm else pltpu.VMEM) for k in range(len(args))
        ],
        out_specs=[
            pl.BlockSpec(memory_space=pltpu.HBM if k in out_hbm else pltpu.VMEM) for k in range(len(outs))
        ],
        scratch_shapes=list(scratch),
        compiler_params=pltpu.CompilerParams(vmem_limit_bytes=32 * 2**20),
        cost_estimate=pl.CostEstimate(flops=flops, bytes_accessed=2 * 2**20, transcendentals=0),
        name=name,
    )(*args)


def exchange(value, axis):
    return lax.all_to_all(value, axis, split_axis=0, concat_axis=0, tiled=True)


def body(features, cotangent, spectral, pointwise, biases):
    table = jnp.asarray(plane_table())
    line = jnp.asarray(line_table())
    piece = ((32, 16, 128), BF16)
    pairs = ((256, 16 * NZ), BF16)
    wide = pltpu.VMEM((C * SLAB * NY, NZ), F32)
    held = pltpu.VMEM(*pairs)
    sem = pltpu.SemaphoreType.DMA(())

    same_core = [[2 * z + core for z in range(8)] for core in range(2)]
    same_chip = [[2 * z, 2 * z + 1] for z in range(8)]
    (copies,) = run(repeat_kernel, "repeat", [((8, 16, 2048), BF16)], [spectral], 10**6,
        [pltpu.VMEM((16, 2048), BF16), pltpu.SemaphoreType.DMA((8,))], (0,),
    )
    blocks = lax.all_to_all(copies, "dp", 0, 0, tiled=True, axis_index_groups=same_core)
    send, x_pairs = run(
        analyse_kernel, "analyse", [piece, pairs], [features.reshape(C * SLAB * NY, NZ), table], 10**9,
        [wide, held, sem], (1,),
    )
    (c_pairs,) = run(
        regroup_kernel, "regroup", [pairs], [cotangent.reshape(C * SLAB * NY, NZ)], 10**6, [wide, held, sem], (0,)
    )
    send, blocks, c_pairs = lax.optimization_barrier((send, blocks, c_pairs))
    w_low, w_high = (
        lax.all_gather(blocks[4 * h : 4 * h + 4], "dp", axis=0, tiled=True, axis_index_groups=same_chip).reshape(128, 2048)
        for h in range(2)
    )
    send, spec = run(
        mix_kernel, "mix", [piece, ((128, 128), F32)], [exchange(send, "space"), w_low, w_high, line], 10**8,
        [pltpu.VMEM((128, 128), F32), sem], (1,),
    )
    bias = jnp.broadcast_to(biases[:, None], (C, 2 * NZ))
    send, delta = run(
        nonlinear_kernel, "nonlinear", [piece, pairs],
        [exchange(send, "space"), table, x_pairs, c_pairs, pointwise, bias], 2 * 10**9,
        [held, held, held, pltpu.VMEM((256, 16 * NZ), F32), pltpu.SemaphoreType.DMA((3, 4))], (1,), (2, 3),
    )
    send, pair = run(
        pull_kernel, "pull", [piece, ((16, 16, 128), BF16)],
        [exchange(send, "space"), w_low, w_high, line, spec], 10**8,
    )
    recv = exchange(send, "space")
    pair, recv = lax.optimization_barrier((pair, recv))
    pair = exchange(pair, "dp")
    (grad_input,) = run(
        input_grad_kernel, "input_grad", [((C * SLAB * NY, NZ), BF16)],
        [recv, table, delta, pointwise], 10**9,
        [wide, held, pltpu.VMEM((C * SLAB * NY, NZ), BF16), pltpu.SemaphoreType.DMA((2, 4))], (0,), (2,),
    )
    (grad_spectral,) = run(weight_grad_kernel, "weight_grad", [((8, 2, 2048), F32)], [pair], 10**8)
    return grad_input.reshape(features.shape), grad_spectral


def solution(mesh):
    placed = (
        P("dp", None, "space", None, None),
        P("dp", None, "space", None, None),
        P("space", "dp", None),
        P(),
        P(),
    )
    return jax.shard_map(
        body,
        mesh=mesh,
        in_specs=placed,
        out_specs=(P("dp", None, "space", None, None), P("space", "dp", None)),
        check_vma=False,
    )
```

```python
import math

import numpy as np
import jax
import jax.numpy as jnp
from jax import lax
from jax.experimental import pallas as pl
from jax.experimental.pallas import tpu as pltpu
from jax.sharding import PartitionSpec as P

KX = 32
KY = 32
KZ = 8
NY = 32
NZ = 128
NX = 128
C = 32
SLAB = 4
STEPS = 15

tanh_coef = 0.7978845608028654
cubic_coef = 0.044715

F32 = jnp.float32
BF16 = jnp.bfloat16


def frequencies(kept_count, length):
    indices = np.arange(kept_count, dtype=np.int32)
    return np.where(indices < kept_count // 2, indices, indices + (length - kept_count)).astype(np.int32)


def plane_table():
    freq_y = frequencies(KY, NY)
    freq_z = np.arange(KZ, dtype=np.int32)
    ys = np.array(list(range(1, 16)) + [0, 16], dtype=np.int32)
    turn_y = ys[:, None] * freq_y[None, :] % NY
    turn_z = np.arange(NZ, dtype=np.int32)[:, None] * freq_z[None, :] % NZ
    angles = np.float32(2.0 * math.pi) * (
        turn_y[:, None, :, None].astype(np.float32) / np.float32(NY)
        + turn_z[None, :, None, :].astype(np.float32) / np.float32(NZ)
    )
    factor = np.float32(1.0 / math.sqrt(NY * NZ))
    table = np.stack([factor * np.cos(angles), -factor * np.sin(angles)], axis=-1)
    table = table.reshape(17, NZ, KY, 2, 4, 2).transpose(2, 4, 3, 5, 0, 1)
    return table.reshape(KY * KZ * 2, 17 * NZ).astype(BF16)


def line_table():
    freq_x = frequencies(KX, NX)
    turns = np.arange(NX, dtype=np.int32)[:, None] * freq_x[None, :] % NX
    angles = np.float32(2.0 * math.pi) * turns.astype(np.float32) / np.float32(NX)
    factor = np.float32(1.0 / math.sqrt(NX))
    cos_part = factor * np.cos(angles)
    sine_part = factor * np.sin(angles)
    first_row = np.stack([cos_part, -sine_part], axis=1)
    second = np.stack([sine_part, cos_part], axis=1)
    line = np.stack([first_row, second], axis=0)
    line = line.reshape(2, 32, 4, 2, 16, 2).transpose(4, 3, 5, 1, 2, 0)
    full = np.zeros((16, 2, 2, 2, 32, 4, 2, 2), np.float32)
    for hi in range(2):
        full[:, :, hi, :, :, :, hi, :] = line
    return full.reshape(128, 512).astype(BF16)


def gelu_slope(values):
    square = values * values
    half = 0.5 + 0.5 * jnp.tanh(values * (tanh_coef + (tanh_coef * cubic_coef) * square))
    return half + (half - half * half) * (values * (2.0 * tanh_coef + (6.0 * tanh_coef * cubic_coef) * square))


def dot(left, right, dims=((1,), (0,))):
    return lax.dot_general(left, right, (dims, ((), ())), preferred_element_type=F32)


def iota(shape, axis):
    return lax.broadcasted_iota(jnp.int32, shape, axis)


def as_bf16(condition):
    return jnp.where(condition, 1.0, 0.0).astype(BF16)


def swap_blocks(value):
    v = value.reshape(64, 8, 128)
    row_low = iota((1, 8, 128), 1) >> 2
    lane = iota((1, 8, 128), 2) >> 5
    lane_low = lane & 1
    lane_high = lane >> 1
    turned = pltpu.roll(v, 4, 1)
    up = pltpu.roll(turned, 32, 2)
    down = pltpu.roll(turned, 96, 2)
    v = jnp.where(row_low == lane_low, v, jnp.where(lane_low == 1, up, down))
    v = v.reshape(32, 2, 8, 128)
    first, second = v[:, 0], v[:, 1]
    new_first = jnp.where(lane_high == 0, first, pltpu.roll(second, 64, 2))
    new_second = jnp.where(lane_high == 1, second, pltpu.roll(first, 64, 2))
    return jnp.stack([new_first, new_second], axis=1).reshape(512, 128)


def negate_jy(value):
    return jnp.concatenate([value[16 * ((32 - j) % 32) : 16 * ((32 - j) % 32) + 16] for j in range(32)], axis=0)


def doubled(value):
    jz = iota(value.shape, 0) & 14
    return value * jnp.where(jz == 0, 1.0, 2.0)


def gather_rows(wide, y):
    return jnp.concatenate(
        [wide[pl.ds(x * NY + y, C, stride=SLAB * NY), :] for x in range(SLAB)], axis=0
    )


def regroup(source_ref, wide, pairs_ref):
    wide[...] = source_ref[...].astype(F32)
    for s in range(1, 17):
        lanes = pl.ds((s - 1) * NZ, NZ)
        above, below = (0, 16) if s == 16 else (s, NY - s)
        pairs_ref[0:128, lanes] = gather_rows(wide, above).astype(BF16)
        pairs_ref[128:256, lanes] = gather_rows(wide, below).astype(BF16)


def to_coarse(table_ref, pairs_ref):
    last = slice(STEPS * NZ, 16 * NZ)
    both = dot(table_ref[:, 0 : STEPS * NZ], pairs_ref[:, 0 : STEPS * NZ], ((1,), (1,)))
    alone = dot(table_ref[:, last], pairs_ref[0:128, last], ((1,), (1,)))
    alone = alone + dot(table_ref[:, 16 * NZ : 17 * NZ], pairs_ref[128:256, last], ((1,), (1,)))
    return alone + both[:, 0:128] + negate_jy(both[:, 128:256])


def analyse_kernel(features_ref, table_ref, send_ref, pairs_out, wide, pairs_ref, sem):
    regroup(features_ref, wide, pairs_ref)
    copy = pltpu.make_async_copy(pairs_ref, pairs_out, sem)
    copy.start()
    coarse = to_coarse(table_ref, pairs_ref)
    send_ref[...] = swap_blocks(coarse).astype(BF16).reshape(32, 16, 128)
    copy.wait()


def regroup_kernel(source_ref, pairs_out, wide, pairs_ref, sem):
    regroup(source_ref, wide, pairs_ref)
    copy = pltpu.make_async_copy(pairs_ref, pairs_out, sem)
    copy.start()
    copy.wait()


def spread_rows():
    row = iota((512, 128), 0)
    block = ((row >> 7) & 1) * 8 + ((row >> 4) & 3) * 2 + ((row >> 6) & 1)
    wanted = block * 8 + (row >> 8) * 4 + ((row >> 3) & 1) * 2 + (row & 1)
    return as_bf16(wanted == iota((512, 128), 1))


def repeat_kernel(spectral_ref, out_hbm, rows_ref, sems):
    rows_ref[...] = jnp.concatenate([spectral_ref[m].astype(F32) for m in range(8)], axis=0).astype(BF16)
    copies = [pltpu.make_async_copy(rows_ref, out_hbm.at[z], sems.at[z]) for z in range(8)]
    for copy in copies:
        copy.start()
    for copy in copies:
        copy.wait()


def weight_columns(low_ref, high_ref, start):
    lanes = slice(start, start + 128)
    return jnp.concatenate([low_ref[:, lanes], high_ref[:, lanes]], axis=0).astype(F32)


def own_lanes(rows):
    row = iota((512, 128), 0)
    return jnp.where((iota((512, 128), 1) >> 5) == ((row >> 1) & 3), rows, 0.0).astype(BF16)


def mix_kernel(recv_ref, low_ref, high_ref, line_ref, send_ref, spec_ref):
    compact = dot(line_ref[...], recv_ref[...].reshape(512, 128)).astype(BF16)
    spec_ref[...] = compact.astype(F32)
    spread = spread_rows()
    rows = own_lanes(dot(spread, compact))
    out_real = jnp.zeros((256, 128), F32)
    out_imag = jnp.zeros((256, 128), F32)
    for t in range(8):
        repeat = as_bf16((iota((128, 128), 0) & 31) == t * 4 + (iota((128, 128), 1) >> 5))
        wide = dot(rows, repeat)
        s_real, s_imag = wide[0:256], wide[256:512]
        w_real = weight_columns(low_ref, high_ref, t * 128)
        w_imag = weight_columns(low_ref, high_ref, 1024 + t * 128)
        out_real = out_real + (s_real * w_real - s_imag * w_imag)
        out_imag = out_imag + (s_real * w_imag + s_imag * w_real)
    mixed = jnp.concatenate([out_real, out_imag], axis=0)
    mixed = mixed + pltpu.roll(mixed, 32, 1)
    mixed = mixed + pltpu.roll(mixed, 64, 1)
    compact = dot(spread, own_lanes(mixed), ((0,), (0,))).astype(BF16)
    send_ref[...] = dot(line_ref[...], compact, ((0,), (0,))).astype(BF16).reshape(32, 16, 128)


def pull_kernel(recv_ref, low_ref, high_ref, line_ref, spec_ref, send_ref, pair_ref):
    compact = dot(line_ref[...], recv_ref[...].reshape(512, 128)).astype(BF16)
    pair_ref[...] = jnp.concatenate(
        [spec_ref[...].reshape(16, 8, 128), compact.astype(F32).reshape(16, 8, 128)], axis=1
    ).astype(BF16)
    spread = spread_rows()
    rows = own_lanes(dot(spread, compact))
    repeat = as_bf16((iota((128, 128), 0) & 31) == (iota((128, 128), 1) & 31))
    wide = dot(rows, repeat)
    a_real, a_imag = wide[0:256], wide[256:512]
    pulled = jnp.zeros((512, 128), F32)
    for t in range(4):
        parts = []
        for u in range(2):
            w_real = weight_columns(low_ref, high_ref, (2 * t + u) * 128)
            w_imag = weight_columns(low_ref, high_ref, 1024 + (2 * t + u) * 128)
            parts.append(
                jnp.concatenate(
                    [a_real * w_real + a_imag * w_imag, a_imag * w_real - a_real * w_imag], axis=0
                ).astype(BF16)
            )
        collect = as_bf16((iota((256, 128), 0) >> 5) + t * 8 == (iota((256, 128), 1) & 31))
        pulled = pulled + dot(jnp.concatenate(parts, axis=1), collect)
    compact = dot(spread, own_lanes(pulled), ((0,), (0,))).astype(BF16)
    send_ref[...] = dot(line_ref[...], compact, ((0,), (0,))).astype(BF16).reshape(32, 16, 128)


def block_weights(weights_ref, transposed):
    spread = as_bf16((iota((256, 32), 0) & 31) == iota((256, 32), 1))
    dims = ((1,), (1,)) if transposed else ((1,), (0,))
    tall = dot(spread, weights_ref[...], dims).astype(BF16)
    full = dot(tall, spread, ((1,), (1,)))
    same = (iota((256, 256), 0) >> 5) == (iota((256, 256), 1) >> 5)
    return jnp.where(same, full, 0.0).astype(BF16), spread


def profiles(recv_ref, scale):
    value = swap_blocks(recv_ref[...].astype(F32).reshape(512, 128))
    if scale:
        value = doubled(value)
    both = jnp.concatenate([value, negate_jy(value)], axis=1)
    return both.T.astype(BF16)


def quarters(source, target, sems):
    width = 4 * NZ
    return [
        pltpu.make_async_copy(
            source.at[:, pl.ds(q * width, width)], target.at[:, pl.ds(q * width, width)], sems.at[q]
        )
        for q in range(4)
    ]


def step_lanes():
    return [(2 * t * NZ, 2 * NZ) for t in range(7)] + [(14 * NZ, NZ)]


def nonlinear_kernel(
    recv_ref, table_ref, x_hbm, c_hbm, weights_ref, bias_ref, send_ref, delta_out, x_ref, c_ref, delta_ref, spec_ref, sems
):
    x_copies = quarters(x_hbm, x_ref, sems.at[0])
    c_copies = quarters(c_hbm, c_ref, sems.at[1])
    out_copies = quarters(delta_ref, delta_out, sems.at[2])
    for q in range(4):
        x_copies[q].start()
        c_copies[q].start()
    basis = profiles(recv_ref, True)
    mixing, spread = block_weights(weights_ref, True)
    bias = dot(spread, bias_ref[...])
    last = slice(STEPS * NZ, 16 * NZ)
    for start, width in step_lanes():
        lanes = slice(start, start + width)
        spec_ref[:, lanes] = dot(basis, table_ref[:, lanes]) + bias[:, 0:width]
    spec_ref[0:128, last] = dot(basis[0:128], table_ref[:, last]) + bias[0:128, 0:NZ]
    spec_ref[128:256, last] = dot(basis[0:128], table_ref[:, 16 * NZ : 17 * NZ]) + bias[128:256, 0:NZ]
    for q in range(4):
        x_copies[q].wait()
        c_copies[q].wait()
        for t in range(2):
            lanes = pl.ds((4 * q + 2 * t) * NZ, 2 * NZ)
            pre = spec_ref[:, lanes] + dot(mixing, x_ref[:, lanes])
            delta_ref[:, lanes] = (c_ref[:, lanes].astype(F32) * gelu_slope(pre)).astype(BF16)
        out_copies[q].start()
    coarse = doubled(to_coarse(table_ref, delta_ref))
    send_ref[...] = swap_blocks(coarse).astype(BF16).reshape(32, 16, 128)
    for copy in out_copies:
        copy.wait()


def input_grad_kernel(recv_ref, table_ref, delta_hbm, weights_ref, out_hbm, wide, delta_ref, out_ref, sems):
    copies = quarters(delta_hbm, delta_ref, sems.at[0])
    for copy in copies:
        copy.start()
    basis = profiles(recv_ref, False)
    mixing, _ = block_weights(weights_ref, False)

    def put(value, y):
        for x in range(SLAB):
            wide[pl.ds(x * NY + y, C, stride=SLAB * NY), :] = value[x * C : x * C + C]

    for t, (start, width) in enumerate(step_lanes()):
        if t % 2 == 0:
            copies[t // 2].wait()
        lanes = slice(start, start + width)
        grad = dot(basis, table_ref[:, lanes]) + dot(mixing, delta_ref[:, lanes])
        for u in range(width // NZ):
            s = start // NZ + u + 1
            put(grad[0:128, u * NZ : u * NZ + NZ], s)
            put(grad[128:256, u * NZ : u * NZ + NZ], NY - s)
    last = slice(STEPS * NZ, 16 * NZ)
    linear = dot(mixing, delta_ref[:, last])
    put(dot(basis[0:128], table_ref[:, last]) + linear[0:128], 0)
    put(dot(basis[0:128], table_ref[:, 16 * NZ : 17 * NZ]) + linear[128:256], 16)
    size = C * SLAB * NY // 4
    copies = []
    for q in range(4):
        rows = pl.ds(q * size, size)
        out_ref[rows, :] = wide[rows, :].astype(BF16)
        copies.append(pltpu.make_async_copy(out_ref.at[rows, :], out_hbm.at[rows, :], sems.at[1, q]))
        copies[q].start()
    for copy in copies:
        copy.wait()


def weight_grad_kernel(pair_ref, out_ref):
    row = iota((64, 16), 0)
    wanted = (row >> 4) * 4 + ((row >> 3) & 1) * 2 + (row & 1)
    select = as_bf16(wanted == iota((64, 16), 1))
    same = (iota((64, 128), 1) >> 5) == ((iota((64, 128), 0) >> 1) & 3)
    rows = [jnp.where(same, dot(select, pair_ref[n]), 0.0).astype(BF16) for n in range(16)]
    rows = jnp.concatenate([rows[n][16 * k : 16 * k + 16] for k in range(4) for n in range(16)], axis=0)
    repeat = as_bf16((iota((128, 128), 0) & 31) == (iota((128, 128), 1) & 31))
    wide = dot(rows[512:1024], repeat)
    a_real, a_imag = wide[0:256], wide[256:512]
    for t in range(8):
        spread = as_bf16((iota((128, 128), 0) & 31) == t * 4 + (iota((128, 128), 1) >> 5))
        wide = dot(rows[0:512], spread)
        s_real, s_imag = wide[0:256], wide[256:512]
        grad_real = jnp.sum((s_real * a_real + s_imag * a_imag).reshape(16, 16, 128), axis=0)
        grad_imag = jnp.sum((s_real * a_imag - s_imag * a_real).reshape(16, 16, 128), axis=0)
        for m in range(8):
            out_ref[m, :, t * 128 : t * 128 + 128] = grad_real[2 * m : 2 * m + 2]
            out_ref[m, :, 1024 + t * 128 : 1024 + t * 128 + 128] = grad_imag[2 * m : 2 * m + 2]


def run(kernel, name, outs, args, flops, scratch=(), out_hbm=(), in_hbm=()):
    args = [pltpu.with_memory_space_constraint(a, pltpu.HBM) if k in in_hbm else a for k, a in enumerate(args)]
    shapes = [(pltpu.HBM if k in out_hbm else jax.ShapeDtypeStruct)(*out) for k, out in enumerate(outs)]
    return pl.pallas_call(
        kernel,
        out_shape=shapes,
        in_specs=[
            pl.BlockSpec(memory_space=pltpu.HBM if k in in_hbm else pltpu.VMEM) for k in range(len(args))
        ],
        out_specs=[
            pl.BlockSpec(memory_space=pltpu.HBM if k in out_hbm else pltpu.VMEM) for k in range(len(outs))
        ],
        scratch_shapes=list(scratch),
        compiler_params=pltpu.CompilerParams(vmem_limit_bytes=32 * 2**20),
        cost_estimate=pl.CostEstimate(flops=flops, bytes_accessed=2 * 2**20, transcendentals=0),
        name=name,
    )(*args)


def exchange(value, axis):
    return lax.all_to_all(value, axis, split_axis=0, concat_axis=0, tiled=True)


def body(features, cotangent, spectral, pointwise, biases):
    table = jnp.asarray(plane_table())
    line = jnp.asarray(line_table())
    piece = ((32, 16, 128), BF16)
    pairs = ((256, 16 * NZ), BF16)
    wide = pltpu.VMEM((C * SLAB * NY, NZ), F32)
    held = pltpu.VMEM(*pairs)
    sem = pltpu.SemaphoreType.DMA(())

    same_core = [[2 * z + core for z in range(8)] for core in range(2)]
    same_chip = [[2 * z, 2 * z + 1] for z in range(8)]
    (copies,) = run(repeat_kernel, "repeat", [((8, 16, 2048), BF16)], [spectral], 10**6,
        [pltpu.VMEM((16, 2048), BF16), pltpu.SemaphoreType.DMA((8,))], (0,),
    )
    blocks = lax.all_to_all(copies, "dp", 0, 0, tiled=True, axis_index_groups=same_core)
    send, x_pairs = run(
        analyse_kernel, "analyse", [piece, pairs], [features.reshape(C * SLAB * NY, NZ), table], 10**9,
        [wide, held, sem], (1,),
    )
    (c_pairs,) = run(
        regroup_kernel, "regroup", [pairs], [cotangent.reshape(C * SLAB * NY, NZ)], 10**6, [wide, held, sem], (0,)
    )
    send, blocks, c_pairs = lax.optimization_barrier((send, blocks, c_pairs))
    w_low, w_high = (
        lax.all_gather(blocks[4 * h : 4 * h + 4], "dp", axis=0, tiled=True, axis_index_groups=same_chip).reshape(128, 2048)
        for h in range(2)
    )
    send, spec = run(
        mix_kernel, "mix", [piece, ((128, 128), F32)], [exchange(send, "space"), w_low, w_high, line], 10**8
    )
    bias = jnp.broadcast_to(biases[:, None], (C, 2 * NZ))
    send, delta = run(
        nonlinear_kernel, "nonlinear", [piece, pairs],
        [exchange(send, "space"), table, x_pairs, c_pairs, pointwise, bias], 2 * 10**9,
        [held, held, held, pltpu.VMEM((256, 16 * NZ), F32), pltpu.SemaphoreType.DMA((3, 4))], (1,), (2, 3),
    )
    send, pair = run(
        pull_kernel, "pull", [piece, ((16, 16, 128), BF16)],
        [exchange(send, "space"), w_low, w_high, line, spec], 10**8,
    )
    recv = exchange(send, "space")
    pair, recv = lax.optimization_barrier((pair, recv))
    pair = exchange(pair, "dp")
    (grad_input,) = run(
        input_grad_kernel, "input_grad", [((C * SLAB * NY, NZ), BF16)],
        [recv, table, delta, pointwise], 10**9,
        [wide, held, pltpu.VMEM((C * SLAB * NY, NZ), BF16), pltpu.SemaphoreType.DMA((2, 4))], (0,), (2,),
    )
    (grad_spectral,) = run(weight_grad_kernel, "weight_grad", [((8, 2, 2048), F32)], [pair], 10**8)
    return grad_input.reshape(features.shape), grad_spectral


def solution(mesh):
    placed = (
        P("dp", None, "space", None, None),
        P("dp", None, "space", None, None),
        P("space", "dp", None),
        P(),
        P(),
    )
    return jax.shard_map(
        body,
        mesh=mesh,
        in_specs=placed,
        out_specs=(P("dp", None, "space", None, None), P("space", "dp", None)),
        check_vma=False,
    )
```
